128 devices in a mesh: seq: 32 (over x, y_hi, z), head: 4 (over y_lo, core).
Axes of the slice: x: 4, y: 4 (y_hi: 2, y_lo: 2; y = y_hi * 2 + y_lo), z: 4, core: 2. Of those that a mesh axis runs over, the one named last changes fastest.
Arguments:
- queries: bfloat16 [2, 16384, 4096], P(None, ('seq', 'head')), may hold values from -6 to 6
- memory_keys: bfloat16 [2, 16384, 4096], P(None, ('seq', 'head')), may hold values from -6 to 6
- memory_values: bfloat16 [2, 16384, 4096], P(None, ('seq', 'head')), may hold values from -6 to 6
- rates: float32 [2, 16384, 8], P(None, ('seq', 'head')), may hold values from 0.001 to 0.01
- fast_gate: float32 [8, 512, 512], P('head'), may hold values from -0.25 to 0.25
- fast_up: float32 [8, 512, 512], P('head'), may hold values from -0.25 to 0.25
- fast_down: float32 [8, 512, 512], P('head'), may hold values from -0.25 to 0.25
Outputs:
- outputs: bfloat16 [2, 16384, 4096], P(None, ('seq', 'head'))
- final_gate: float32 [8, 512, 512], P('head')
- final_up: float32 [8, 512, 512], P('head')
- final_down: float32 [8, 512, 512], P('head')
The draws below stay inside these ranges and needn't reach their ends.
All inputs are finite; a program needn't handle non-finite values.
Results may differ from the reference program's by a relative error of at most 0.035.
Values may be sent and summed in bfloat16 or wider, within the bound.
A program may use at most 128 MiB of HBM per device.

```python
import math
import jax
import jax.numpy as jnp
from jax import lax

HEADS = 8
HD = 512
FH = 512
SPANS = 2
D = 4096
TOKENS = 16384


def steps_of(own_key, dims, split, low, high):
    loudness = 1.0
    for axis_at, shards_of in split:
        draws = jax.random.uniform(jax.random.fold_in(jax.random.fold_in(own_key, 6), axis_at), (shards_of,), jnp.float32, low / len(split), high / len(split))
        loudness = loudness * jnp.repeat(jnp.exp(draws), dims[axis_at] // shards_of).reshape((-1,) + (1,) * (len(dims) - 1 - axis_at))
    return loudness


def normal_values(stream_key, extent, deviation, limit, split=(), kind=jnp.bfloat16):
    entries = jax.random.normal(stream_key, extent, jnp.float32) * deviation
    if len(split) > 0:
        entries = steps_of(stream_key, extent, split, -0.22, 0.18) * entries
    return jnp.clip(entries, min=-limit, max=limit).astype(kind)


def setup_inputs(seed: int = 0) -> dict:
    key_of = jax.random.split(jax.random.key(seed), 8)
    queries = normal_values(key_of[0], (SPANS, TOKENS, D), 1.0, 6.0, ((1, 128),))
    memory_keys = normal_values(key_of[1], (SPANS, TOKENS, D), 1.0, 6.0, ((1, 128),))
    memory_values = normal_values(key_of[2], (SPANS, TOKENS, D), 1.0, 6.0, ((1, 128),))
    rates = jnp.clip(jnp.exp(math.log(0.01) - 2.30258502 * jax.random.uniform(key_of[3], (SPANS, TOKENS, HEADS), jnp.float32) ** steps_of(key_of[3], (SPANS, TOKENS, HEADS), ((1, 128),), -0.2, 0.2)), 0.001, 0.01)
    fast_gate = normal_values(key_of[4], (HEADS, HD, FH), HD ** -0.5, 0.25, ((0, 4),), jnp.float32)
    fast_up = normal_values(key_of[5], (HEADS, HD, FH), HD ** -0.5, 0.25, ((0, 4),), jnp.float32)
    fast_down = normal_values(key_of[6], (HEADS, FH, HD), FH ** -0.5, 0.25, ((0, 4),), jnp.float32)
    return {"queries": queries, "memory_keys": memory_keys, "memory_values": memory_values, "rates": rates, "fast_gate": fast_gate, "fast_up": fast_up, "fast_down": fast_down}


EPSILON = 1e-06

def head_gradients(gate_weight, up_weight, down_weight, key_block, value_block, rate_block):
    gate_half = gate_weight.astype(jnp.bfloat16)
    up_half = up_weight.astype(jnp.bfloat16)
    down_half = down_weight.astype(jnp.bfloat16)
    gate_pre = jnp.dot(key_block, gate_half, preferred_element_type=jnp.float32)
    up_pre = jnp.dot(key_block, up_half, preferred_element_type=jnp.float32)
    sigmoid_gate = jax.nn.sigmoid(gate_pre)
    activated = gate_pre * sigmoid_gate
    hidden = (activated * up_pre).astype(jnp.bfloat16)
    target = (-rate_block[:, None] * value_block.astype(jnp.float32)).astype(jnp.bfloat16)
    grad_down = jnp.dot(hidden.T, target, preferred_element_type=jnp.float32)
    hidden_grad = jnp.dot(target, down_half.T, preferred_element_type=jnp.float32)
    gate_delta = (hidden_grad * up_pre * sigmoid_gate * (1.0 + gate_pre * (1.0 - sigmoid_gate))).astype(jnp.bfloat16)
    up_delta = (hidden_grad * activated).astype(jnp.bfloat16)
    grad_gate = jnp.dot(key_block.T, gate_delta, preferred_element_type=jnp.float32)
    grad_up = jnp.dot(key_block.T, up_delta, preferred_element_type=jnp.float32)
    return (grad_gate, grad_up, grad_down)

def renormalize(weight, gradient):
    updated = weight - gradient
    old_norm = jnp.sqrt(lax.optimization_barrier(jnp.sum(weight * weight, axis=-2, keepdims=True)) + EPSILON)
    new_norm = jnp.sqrt(lax.optimization_barrier(jnp.sum(updated * updated, axis=-2, keepdims=True)) + EPSILON)
    return updated * (old_norm / new_norm)

def apply_head(gate_weight, up_weight, down_weight, query_block):
    gate_pre = jnp.dot(query_block, gate_weight.astype(jnp.bfloat16), preferred_element_type=jnp.float32)
    up_pre = jnp.dot(query_block, up_weight.astype(jnp.bfloat16), preferred_element_type=jnp.float32)
    hidden = (jax.nn.silu(gate_pre) * up_pre).astype(jnp.bfloat16)
    return jnp.dot(hidden, down_weight.astype(jnp.bfloat16), preferred_element_type=jnp.float32).astype(jnp.bfloat16)

def reference(queries, memory_keys, memory_values, rates, fast_gate, fast_up, fast_down):
    gate_state, up_state, down_state = (fast_gate, fast_up, fast_down)
    results = []
    for block_index in range(SPANS):
        key_heads = memory_keys[block_index].reshape(TOKENS, HEADS, HD)
        value_heads = memory_values[block_index].reshape(TOKENS, HEADS, HD)
        query_heads = queries[block_index].reshape(TOKENS, HEADS, HD)
        grad_gate, grad_up, grad_down = jax.vmap(head_gradients, in_axes=(0, 0, 0, 1, 1, 1))(gate_state, up_state, down_state, key_heads, value_heads, rates[block_index])
        gate_state = renormalize(gate_state, grad_gate)
        up_state = renormalize(up_state, grad_up)
        down_state = renormalize(down_state, grad_down)
        applied = jax.vmap(apply_head, in_axes=(0, 0, 0, 1), out_axes=1)(gate_state, up_state, down_state, query_heads)
        results.append(applied.reshape(TOKENS, D))
    return (jnp.stack(results), gate_state, up_state, down_state)
```

```python
import jax
import jax.numpy as jnp
from jax import lax
from jax.experimental import pallas as pl
from jax.experimental.pallas import tpu as pltpu
from jax.sharding import PartitionSpec as P

EPSILON = 1e-06
MESH = pl.DeviceIdType.MESH
F32 = jnp.float32
BF16 = jnp.bfloat16
GATE, UP, DOWN = 0, 1, 2
NEAR = (2, 1, 3)


def nt(a, b):
    return lax.dot_general(a, b, (((1,), (1,)), ((), ())), preferred_element_type=F32)


def nn(a, b):
    return lax.dot_general(a, b, (((1,), (0,)), ((), ())), preferred_element_type=F32)


def tn(a, b):
    return lax.dot_general(a, b, (((0,), (0,)), ((), ())), preferred_element_type=F32)


def device(x, y, z, core):
    return {"seq": x * 8 + (y // 2) * 4 + z, "head": (y % 2) * 2 + core}


def head_of(y, core):
    return 4 * (y % 2) + 2 * core + y // 2


def kernel(
    q, k, v, r, g, u, w, out, fin,
    kb, tb, qb, vb, tl, wf, st, wt, hid, ga, gb, da, db, gf, gs, r1, pf, s2, r2, wo, ob,
    tok_s, tok_r, out_s, out_r, rs1_s, rs1_r, rs2_s, rs2_r, ag1_s, ag1_r, ag2_s, ag2_r,
    fx_s, fx_r, fa1_s, fa1_r, fa2_s, fa2_r, loc,
):
    seq, hd = lax.axis_index("seq"), lax.axis_index("head")
    x, z = seq // 8, seq % 4
    y = ((seq // 4) % 2) * 2 + hd // 2
    core = hd % 2
    me = y * 2 + core
    head = head_of(y, core)
    sends = []

    def put(src, dst, ssem, rsem, where):
        copy = pltpu.make_async_remote_copy(
            src_ref=src, dst_ref=dst, send_sem=ssem, recv_sem=rsem, device_id=where, device_id_type=MESH
        )
        copy.start()
        sends.append(copy)
        return copy

    def local(src, dst, n):
        copy = pltpu.make_async_copy(src, dst, loc.at[n])
        copy.start()
        return copy

    def cols(h):
        return pl.ds(pl.multiple_of(h * 512, 512), 512)

    def rows(start, size):
        return pl.ds(pl.multiple_of(start, size), size)

    own_v = [local(v.at[c], vb.at[c], c) for c in range(2)]
    own_w = [local(m.at[y // 2], wf.at[n], 2 + n) for n, m in enumerate((g, u, w))]
    own_k = [local(k.at[c, :, cols(head)], kb.at[c, rows(me * 128, 128), :], 5 + c) for c in range(2)]
    own_q = [local(q.at[c, :, cols(head)], qb.at[c, rows(me * 128, 128), :], 7 + c) for c in range(2)]

    group = [(dy, dc) for dy in NEAR for dc in range(2)] + [(0, 1)]
    friends = [device(x, (y + dy) % 4, z, (core + dc) % 2) for dy, dc in group]
    friends += [device((x + d) % 4, y, z, core) for d in NEAR]
    friends += [device(x, y, (z + d) % 4, core) for d in NEAR]
    barrier = pltpu.get_barrier_semaphore()
    for where in friends:
        pl.semaphore_signal(barrier, inc=1, device_id=where, device_id_type=MESH)
    pl.semaphore_wait(barrier, len(friends))

    def send_tokens(c, kind, source, held):
        copies = []
        for dy, dc in group:
            y2, core2 = (y + dy) % 4, (core + dc) % 2
            n = dy * 2 + dc - 1
            copies.append(
                put(
                    source(head_of(y2, core2)),
                    held.at[c, rows(me * 128, 128), :],
                    tok_s.at[c, kind, n],
                    tok_r.at[c, kind, n],
                    device(x, y2, z, core2),
                )
            )
        return copies

    def targets(c):
        own_v[c].wait()
        for h in range(8):
            tl[c, h] = (-r[c, :, h : h + 1] * vb[c, :, h * 512 : (h + 1) * 512].astype(F32)).astype(BF16)
        tb[c, rows(me * 128, 128), :] = tl[c, head]

    got_k, got_t, got_q = [None, None], [None, None], [None, None]
    for c in range(2):
        got_k[c] = send_tokens(c, 0, lambda h: k.at[c, :, cols(h)], kb)
        targets(c)
        got_t[c] = send_tokens(c, 1, lambda h: tl.at[c, h], tb)
        got_q[c] = send_tokens(c, 2, lambda h: q.at[c, :, cols(h)], qb)

    first = (x, z)
    second = (z, x)
    share = [256 * p + 64 * first[p] + 16 * second[p] for p in range(2)]

    def along(p, phase, d):
        if (p + phase) % 2 == 0:
            return device((x + d) % 4, y, z, core)
        return device(x, y, (z + d) % 4, core)

    for n in range(3):
        own_w[n].wait()
        turned = wf[n].T
        gf[n] = turned
        wt[0, n] = turned.astype(BF16)
        for p in range(2):
            st[n, p] = gf[n, rows(share[p], 16), :]

    def reduce_out(c, m, p):
        copies = []
        for d in NEAR:
            src = gs.at[c, m, rows(256 * p + 64 * ((first[p] + d) % 4), 64), :]
            copies.append(
                put(src, r1.at[c, m, p, d - 1], rs1_s.at[c, m, p, d - 1], rs1_r.at[c, m, p, d - 1], along(p, 0, d))
            )
        return copies

    def reduce_mid(c, m, p, waits):
        for copy in waits:
            copy.wait_recv()
        total = gf[m, rows(256 * p + 64 * first[p], 64), :]
        for d in range(3):
            total = total + r1[c, m, p, d].astype(F32)
        pf[m, p] = total
        s2[c, m, p] = total.astype(BF16)
        copies = []
        for d in NEAR:
            src = s2.at[c, m, p, rows(16 * ((second[p] + d) % 4), 16), :]
            copies.append(
                put(src, r2.at[c, m, p, d - 1], rs2_s.at[c, m, p, d - 1], rs2_r.at[c, m, p, d - 1], along(p, 1, d))
            )
        return copies

    def update(c, m, p, waits):
        for copy in waits:
            copy.wait_recv()
        grad = pf[m, p, rows(16 * second[p], 16), :]
        for d in range(3):
            grad = grad + r2[c, m, p, d].astype(F32)
        old = st[m, p]
        new = old - grad
        old_norm = jnp.sqrt(jnp.sum(old * old, axis=1, keepdims=True) + EPSILON)
        new_norm = jnp.sqrt(jnp.sum(new * new, axis=1, keepdims=True) + EPSILON)
        new = new * (old_norm / new_norm)
        st[m, p] = new
        part = rows(share[p], 16)
        wt[c + 1, m, part, :] = new.astype(BF16)
        copies = []
        for d in NEAR:
            piece = wt.at[c + 1, m, part, :]
            copies.append(put(piece, piece, ag1_s.at[c, m, p, d - 1], ag1_r.at[c, m, p, d - 1], along(p, 1, d)))
        return copies

    def spread(c, m, p, waits):
        for copy in waits:
            copy.wait_recv()
        copies = []
        for d in NEAR:
            piece = wt.at[c + 1, m, rows(256 * p + 64 * first[p], 64), :]
            copies.append(put(piece, piece, ag2_s.at[c, m, p, d - 1], ag2_r.at[c, m, p, d - 1], along(p, 0, d)))
        return copies

    def both(step, c, m, waits=None):
        if waits is None:
            return [step(c, m, p) for p in range(2)]
        return [step(c, m, p, waits[p]) for p in range(2)]

    def arrived(copies):
        for part in copies:
            for copy in part:
                copy.wait_recv()

    def forward(c):
        own_k[c].wait()
        for copy in got_k[c]:
            copy.wait_recv()

        def block(i, _):
            part = rows(i * 256, 256)
            keys = kb[c, part, :]
            a = nt(keys, wt[c, GATE])
            b = nt(keys, wt[c, UP])
            s = jax.nn.sigmoid(a)
            act = a * s
            hid[part, :] = (act * b).astype(BF16)
            ga[part, :] = b * s * (1.0 + a * (1.0 - s))
            gb[part, :] = act
            return 0

        lax.fori_loop(0, 4, block, 0)

    def grad_half(c, m, p, left, right):
        res = tn(left[:, 256 * p : 256 * (p + 1)], right)
        gf[m, 256 * p : 256 * (p + 1), :] = res
        gs[c, m, 256 * p : 256 * (p + 1), :] = res.astype(BF16)
        return reduce_out(c, m, p)

    def deltas(c):
        def block(i, _):
            part = rows(i * 256, 256)
            dh = nn(tb[c, part, :], wt[c, DOWN])
            da[part, :] = (dh * ga[part, :]).astype(BF16)
            db[part, :] = (dh * gb[part, :]).astype(BF16)
            return 0

        lax.fori_loop(0, 4, block, 0)

    kept = []

    def apply_block(c, dy):
        y2 = (y + dy) % 4
        part = rows(256 * y2, 256)
        queries = qb[c, part, :]
        p = nt(queries, wt[c + 1, GATE])
        u2 = nt(queries, wt[c + 1, UP])
        hidden = (p * jax.nn.sigmoid(p) * u2).astype(BF16)
        ob[c, part, :] = nt(hidden, wt[c + 1, DOWN]).astype(BF16)
        copies = []
        for dc in range(2):
            core2 = (core + dc) % 2
            tile = ob.at[c, rows(256 * y2 + 128 * core2, 128), :]
            place = out.at[c, :, cols(head)]
            if dy == 0 and dc == 0:
                kept.append(local(tile, place, 9 + c))
            else:
                n = dy * 2 + dc - 1
                copies.append(put(tile, place, out_s.at[c, n], out_r.at[c, n], device(x, y2, z, core2)))
        return copies

    got_out = []

    def apply_all(c):
        own_q[c].wait()
        for copy in got_q[c]:
            copy.wait_recv()
        for dy in NEAR + (0,):
            got_out.extend(apply_block(c, dy))

    def other_exchange():
        copies = []
        for p in range(2):
            part = rows(share[p], 16)
            copies.append(
                put(wt.at[2, :, part, :], wo.at[:, part, :], fx_s.at[p], fx_r.at[p], device(x, (y + 2) % 4, z, core))
            )
        return copies

    def other_first(waits):
        copies = []
        for p in range(2):
            waits[p].wait_recv()
            piece = wo.at[:, rows(share[p], 16), :]
            copies.append(
                [put(piece, piece, fa1_s.at[p, d - 1], fa1_r.at[p, d - 1], along(p, 1, d)) for d in NEAR]
            )
        return copies

    def other_second(waits):
        copies = []
        for p in range(2):
            for copy in waits[p]:
                copy.wait_recv()
            piece = wo.at[:, rows(256 * p + 64 * first[p], 64), :]
            copies.append(
                [put(piece, piece, fa2_s.at[p, d - 1], fa2_r.at[p, d - 1], along(p, 0, d)) for d in NEAR]
            )
        return copies

    for c in range(2):
        forward(c)
        for copy in got_t[c]:
            copy.wait_recv()
        w1 = [grad_half(c, DOWN, p, tb.at[c], hid[...]) for p in range(2)]
        deltas(c)
        g1 = [grad_half(c, GATE, p, da, kb[c]) for p in range(2)]
        w2 = both(reduce_mid, c, DOWN, w1)
        u1 = [grad_half(c, UP, p, db, kb[c]) for p in range(2)]
        g2 = both(reduce_mid, c, GATE, g1)
        w3 = both(update, c, DOWN, w2)
        if c == 1:
            apply_all(0)
        u2 = both(reduce_mid, c, UP, u1)
        g3 = both(update, c, GATE, g2)
        w4 = both(spread, c, DOWN, w3)
        u3 = both(update, c, UP, u2)
        if c == 1:
            fx = other_exchange()
        g4 = both(spread, c, GATE, g3)
        u4 = both(spread, c, UP, u3)
        if c == 1:
            f1 = other_first(fx)
        arrived(g4)
        arrived(u4)
        arrived(w4)
    apply_all(1)
    f2 = other_second(f1)
    for n in range(3):
        fin[n, y // 2] = wt[2, n].astype(F32).T.astype(BF16)
    arrived(f2)
    for n in range(3):
        fin[n, 1 - y // 2] = wo[n].astype(F32).T.astype(BF16)
    for copy in got_out:
        copy.wait_recv()
    for copy in kept:
        copy.wait()
    for copy in sends:
        copy.wait_send()


def on_device(queries, memory_keys, memory_values, rates, fast_gate, fast_up, fast_down):
    anywhere = pl.BlockSpec(memory_space=pl.ANY)
    inside = pl.BlockSpec(memory_space=pltpu.VMEM)
    dma = pltpu.SemaphoreType.DMA
    tokens = pltpu.VMEM((2, 1024, 512), BF16)
    plain = pltpu.VMEM((1024, 512), BF16)
    wide = pltpu.VMEM((1024, 512), F32)
    out, fin = pl.pallas_call(
        kernel,
        name="fast_weights",
        out_shape=(
            jax.ShapeDtypeStruct((2, 128, 4096), BF16),
            jax.ShapeDtypeStruct((3, 2, 512, 512), BF16),
        ),
        in_specs=[anywhere, anywhere, anywhere, inside, anywhere, anywhere, anywhere],
        out_specs=(anywhere, inside),
        scratch_shapes=[
            tokens, tokens, tokens,
            pltpu.VMEM((2, 128, 4096), BF16),
            pltpu.VMEM((2, 8, 128, 512), BF16),
            pltpu.VMEM((3, 512, 512), F32),
            pltpu.VMEM((3, 2, 16, 512), F32),
            pltpu.VMEM((3, 3, 512, 512), BF16),
            plain, wide, wide, plain, plain,
            pltpu.VMEM((3, 512, 512), F32),
            pltpu.VMEM((2, 3, 512, 512), BF16),
            pltpu.VMEM((2, 3, 2, 3, 64, 512), BF16),
            pltpu.VMEM((3, 2, 64, 512), F32),
            pltpu.VMEM((2, 3, 2, 64, 512), BF16),
            pltpu.VMEM((2, 3, 2, 3, 16, 512), BF16),
            pltpu.VMEM((3, 512, 512), BF16),
            tokens,
            dma((2, 3, 7)), dma((2, 3, 7)),
            dma((2, 7)), dma((2, 7)),
            dma((2, 3, 2, 3)), dma((2, 3, 2, 3)),
            dma((2, 3, 2, 3)), dma((2, 3, 2, 3)),
            dma((2, 3, 2, 3)), dma((2, 3, 2, 3)),
            dma((2, 3, 2, 3)), dma((2, 3, 2, 3)),
            dma((2,)), dma((2,)),
            dma((2, 3)), dma((2, 3)),
            dma((2, 3)), dma((2, 3)),
            dma((11,)),
        ],
        compiler_params=pltpu.CompilerParams(
            collective_id=0, has_side_effects=True, vmem_limit_bytes=60 << 20
        ),
    )(queries, memory_keys, memory_values, rates, fast_gate, fast_up, fast_down)
    state = fin.astype(F32)
    return out, state[0], state[1], state[2]


def solution(mesh):
    tokens = P(None, ("seq", "head"), None)
    heads = P("head", None, None)
    return jax.shard_map(
        on_device,
        mesh=mesh,
        in_specs=(tokens, tokens, tokens, tokens, heads, heads, heads),
        out_specs=(tokens, heads, heads, heads),
        check_vma=False,
    )
```

```python
import jax
import jax.numpy as jnp
from jax import lax
from jax.experimental import pallas as pl
from jax.experimental.pallas import tpu as pltpu
from jax.sharding import PartitionSpec as P

EPSILON = 1e-06
MESH = pl.DeviceIdType.MESH
F32 = jnp.float32
BF16 = jnp.bfloat16
GATE, UP, DOWN = 0, 1, 2
NEAR = (2, 1, 3)


def nt(a, b):
    return lax.dot_general(a, b, (((1,), (1,)), ((), ())), preferred_element_type=F32)


def nn(a, b):
    return lax.dot_general(a, b, (((1,), (0,)), ((), ())), preferred_element_type=F32)


def tn(a, b):
    return lax.dot_general(a, b, (((0,), (0,)), ((), ())), preferred_element_type=F32)


def device(x, y, z, core):
    return {"seq": x * 8 + (y // 2) * 4 + z, "head": (y % 2) * 2 + core}


def head_of(y, core):
    return 4 * (y % 2) + 2 * core + y // 2


def kernel(
    q, k, v, r, g, u, w, out, fin,
    kb, tb, qb, vb, tl, wf, st, wt, hid, ga, gb, da, db, gf, gs, r1, pf, s2, r2, wo, ob,
    tok_s, tok_r, out_s, out_r, rs1_s, rs1_r, rs2_s, rs2_r, ag1_s, ag1_r, ag2_s, ag2_r,
    fx_s, fx_r, fa1_s, fa1_r, fa2_s, fa2_r, loc,
):
    seq, hd = lax.axis_index("seq"), lax.axis_index("head")
    x, z = seq // 8, seq % 4
    y = ((seq // 4) % 2) * 2 + hd // 2
    core = hd % 2
    me = y * 2 + core
    head = head_of(y, core)
    sends = []

    def put(src, dst, ssem, rsem, where):
        copy = pltpu.make_async_remote_copy(
            src_ref=src, dst_ref=dst, send_sem=ssem, recv_sem=rsem, device_id=where, device_id_type=MESH
        )
        copy.start()
        sends.append(copy)
        return copy

    def local(src, dst, n):
        copy = pltpu.make_async_copy(src, dst, loc.at[n])
        copy.start()
        return copy

    def cols(h):
        return pl.ds(pl.multiple_of(h * 512, 512), 512)

    def rows(start, size):
        return pl.ds(pl.multiple_of(start, size), size)

    own_v = [local(v.at[c], vb.at[c], c) for c in range(2)]
    own_w = [local(m.at[y // 2], wf.at[n], 2 + n) for n, m in enumerate((g, u, w))]
    own_k = [local(k.at[c, :, cols(head)], kb.at[c, rows(me * 128, 128), :], 5 + c) for c in range(2)]
    own_q = [local(q.at[c, :, cols(head)], qb.at[c, rows(me * 128, 128), :], 7 + c) for c in range(2)]

    group = [(dy, dc) for dy in NEAR for dc in range(2)] + [(0, 1)]
    friends = [device(x, (y + dy) % 4, z, (core + dc) % 2) for dy, dc in group]
    friends += [device((x + d) % 4, y, z, core) for d in NEAR]
    friends += [device(x, y, (z + d) % 4, core) for d in NEAR]
    barrier = pltpu.get_barrier_semaphore()
    for where in friends:
        pl.semaphore_signal(barrier, inc=1, device_id=where, device_id_type=MESH)
    pl.semaphore_wait(barrier, len(friends))

    def send_tokens(c, kind, source, held):
        copies = []
        for dy, dc in group:
            y2, core2 = (y + dy) % 4, (core + dc) % 2
            n = dy * 2 + dc - 1
            copies.append(
                put(
                    source(head_of(y2, core2)),
                    held.at[c, rows(me * 128, 128), :],
                    tok_s.at[c, kind, n],
                    tok_r.at[c, kind, n],
                    device(x, y2, z, core2),
                )
            )
        return copies

    def targets(c):
        rate = r[c].T
        own_v[c].wait()
        for h in range(8):
            tl[c, h] = (-rate[:, h : h + 1] * vb[c, :, h * 512 : (h + 1) * 512].astype(F32)).astype(BF16)
        tb[c, rows(me * 128, 128), :] = tl[c, head]

    got_k, got_t, got_q = [None, None], [None, None], [None, None]
    for c in range(2):
        got_k[c] = send_tokens(c, 0, lambda h: k.at[c, :, cols(h)], kb)
        targets(c)
        got_t[c] = send_tokens(c, 1, lambda h: tl.at[c, h], tb)
        got_q[c] = send_tokens(c, 2, lambda h: q.at[c, :, cols(h)], qb)

    first = (x, z)
    second = (z, x)
    share = [256 * p + 64 * first[p] + 16 * second[p] for p in range(2)]

    def along(p, phase, d):
        if (p + phase) % 2 == 0:
            return device((x + d) % 4, y, z, core)
        return device(x, y, (z + d) % 4, core)

    for n in range(3):
        own_w[n].wait()
        turned = wf[n].T
        gf[n] = turned
        wt[0, n] = turned.astype(BF16)
        for p in range(2):
            st[n, p] = gf[n, rows(share[p], 16), :]

    def reduce_out(c, m, p):
        copies = []
        for d in NEAR:
            src = gs.at[c, m, rows(256 * p + 64 * ((first[p] + d) % 4), 64), :]
            copies.append(
                put(src, r1.at[c, m, p, d - 1], rs1_s.at[c, m, p, d - 1], rs1_r.at[c, m, p, d - 1], along(p, 0, d))
            )
        return copies

    def reduce_mid(c, m, p, waits):
        for copy in waits:
            copy.wait_recv()
        total = gf[m, rows(256 * p + 64 * first[p], 64), :]
        for d in range(3):
            total = total + r1[c, m, p, d].astype(F32)
        pf[m, p] = total
        s2[c, m, p] = total.astype(BF16)
        copies = []
        for d in NEAR:
            src = s2.at[c, m, p, rows(16 * ((second[p] + d) % 4), 16), :]
            copies.append(
                put(src, r2.at[c, m, p, d - 1], rs2_s.at[c, m, p, d - 1], rs2_r.at[c, m, p, d - 1], along(p, 1, d))
            )
        return copies

    def update(c, m, p, waits):
        for copy in waits:
            copy.wait_recv()
        grad = pf[m, p, rows(16 * second[p], 16), :]
        for d in range(3):
            grad = grad + r2[c, m, p, d].astype(F32)
        old = st[m, p]
        new = old - grad
        old_norm = jnp.sqrt(jnp.sum(old * old, axis=1, keepdims=True) + EPSILON)
        new_norm = jnp.sqrt(jnp.sum(new * new, axis=1, keepdims=True) + EPSILON)
        new = new * (old_norm / new_norm)
        st[m, p] = new
        part = rows(share[p], 16)
        wt[c + 1, m, part, :] = new.astype(BF16)
        copies = []
        for d in NEAR:
            piece = wt.at[c + 1, m, part, :]
            copies.append(put(piece, piece, ag1_s.at[c, m, p, d - 1], ag1_r.at[c, m, p, d - 1], along(p, 1, d)))
        return copies

    def spread(c, m, p, waits):
        for copy in waits:
            copy.wait_recv()
        copies = []
        for d in NEAR:
            piece = wt.at[c + 1, m, rows(256 * p + 64 * first[p], 64), :]
            copies.append(put(piece, piece, ag2_s.at[c, m, p, d - 1], ag2_r.at[c, m, p, d - 1], along(p, 0, d)))
        return copies

    def both(step, c, m, waits=None):
        if waits is None:
            return [step(c, m, p) for p in range(2)]
        return [step(c, m, p, waits[p]) for p in range(2)]

    def arrived(copies):
        for part in copies:
            for copy in part:
                copy.wait_recv()

    def forward(c):
        own_k[c].wait()
        for copy in got_k[c]:
            copy.wait_recv()

        def block(i, _):
            part = rows(i * 256, 256)
            keys = kb[c, part, :]
            a = nt(keys, wt[c, GATE])
            b = nt(keys, wt[c, UP])
            s = jax.nn.sigmoid(a)
            act = a * s
            hid[part, :] = (act * b).astype(BF16)
            ga[part, :] = b * s * (1.0 + a * (1.0 - s))
            gb[part, :] = act
            return 0

        lax.fori_loop(0, 4, block, 0)

    def grad_half(c, m, p, left, right):
        res = tn(left[:, 256 * p : 256 * (p + 1)], right)
        gf[m, 256 * p : 256 * (p + 1), :] = res
        gs[c, m, 256 * p : 256 * (p + 1), :] = res.astype(BF16)
        return reduce_out(c, m, p)

    def deltas(c):
        def block(i, _):
            part = rows(i * 256, 256)
            dh = nn(tb[c, part, :], wt[c, DOWN])
            da[part, :] = (dh * ga[part, :]).astype(BF16)
            db[part, :] = (dh * gb[part, :]).astype(BF16)
            return 0

        lax.fori_loop(0, 4, block, 0)

    kept = []

    def apply_block(c, dy):
        y2 = (y + dy) % 4
        part = rows(256 * y2, 256)
        queries = qb[c, part, :]
        p = nt(queries, wt[c + 1, GATE])
        u2 = nt(queries, wt[c + 1, UP])
        hidden = (p * jax.nn.sigmoid(p) * u2).astype(BF16)
        ob[c, part, :] = nt(hidden, wt[c + 1, DOWN]).astype(BF16)
        copies = []
        for dc in range(2):
            core2 = (core + dc) % 2
            tile = ob.at[c, rows(256 * y2 + 128 * core2, 128), :]
            place = out.at[c, :, cols(head)]
            if dy == 0 and dc == 0:
                kept.append(local(tile, place, 9 + c))
            else:
                n = dy * 2 + dc - 1
                copies.append(put(tile, place, out_s.at[c, n], out_r.at[c, n], device(x, y2, z, core2)))
        return copies

    got_out = []

    def apply_all(c):
        own_q[c].wait()
        for copy in got_q[c]:
            copy.wait_recv()
        for dy in NEAR + (0,):
            got_out.extend(apply_block(c, dy))

    def other_exchange():
        copies = []
        for p in range(2):
            part = rows(share[p], 16)
            copies.append(
                put(wt.at[2, :, part, :], wo.at[:, part, :], fx_s.at[p], fx_r.at[p], device(x, (y + 2) % 4, z, core))
            )
        return copies

    def other_first(waits):
        copies = []
        for p in range(2):
            waits[p].wait_recv()
            piece = wo.at[:, rows(share[p], 16), :]
            copies.append(
                [put(piece, piece, fa1_s.at[p, d - 1], fa1_r.at[p, d - 1], along(p, 1, d)) for d in NEAR]
            )
        return copies

    def other_second(waits):
        copies = []
        for p in range(2):
            for copy in waits[p]:
                copy.wait_recv()
            piece = wo.at[:, rows(256 * p + 64 * first[p], 64), :]
            copies.append(
                [put(piece, piece, fa2_s.at[p, d - 1], fa2_r.at[p, d - 1], along(p, 0, d)) for d in NEAR]
            )
        return copies

    def ready(c):
        if c == 1:
            own_q[0].wait()
            for copy in got_q[0]:
                copy.wait_recv()

    def piece_of(c, dy):
        if c == 1:
            got_out.extend(apply_block(0, dy))

    for c in range(2):
        forward(c)
        for copy in got_t[c]:
            copy.wait_recv()
        w1 = [grad_half(c, DOWN, p, tb.at[c], hid[...]) for p in range(2)]
        deltas(c)
        g1 = [grad_half(c, GATE, p, da, kb[c]) for p in range(2)]
        w2 = both(reduce_mid, c, DOWN, w1)
        u1 = [grad_half(c, UP, p, db, kb[c]) for p in range(2)]
        ready(c)
        g2 = both(reduce_mid, c, GATE, g1)
        piece_of(c, 2)
        w3 = both(update, c, DOWN, w2)
        piece_of(c, 1)
        u2 = both(reduce_mid, c, UP, u1)
        piece_of(c, 3)
        g3 = both(update, c, GATE, g2)
        piece_of(c, 0)
        w4 = both(spread, c, DOWN, w3)
        u3 = both(update, c, UP, u2)
        if c == 1:
            fx = other_exchange()
        g4 = both(spread, c, GATE, g3)
        u4 = both(spread, c, UP, u3)
        if c == 1:
            f1 = other_first(fx)
        arrived(g4)
        arrived(u4)
        arrived(w4)
    apply_all(1)
    f2 = other_second(f1)
    for n in range(3):
        fin[n, y // 2] = wt[2, n].astype(F32).T.astype(BF16)
    arrived(f2)
    for n in range(3):
        fin[n, 1 - y // 2] = wo[n].astype(F32).T.astype(BF16)
    for copy in got_out:
        copy.wait_recv()
    for copy in kept:
        copy.wait()
    for copy in sends:
        copy.wait_send()


def on_device(queries, memory_keys, memory_values, rates, fast_gate, fast_up, fast_down):
    anywhere = pl.BlockSpec(memory_space=pl.ANY)
    inside = pl.BlockSpec(memory_space=pltpu.VMEM)
    dma = pltpu.SemaphoreType.DMA
    tokens = pltpu.VMEM((2, 1024, 512), BF16)
    plain = pltpu.VMEM((1024, 512), BF16)
    wide = pltpu.VMEM((1024, 512), F32)
    out, fin = pl.pallas_call(
        kernel,
        name="fast_weights",
        out_shape=(
            jax.ShapeDtypeStruct((2, 128, 4096), BF16),
            jax.ShapeDtypeStruct((3, 2, 512, 512), BF16),
        ),
        in_specs=[anywhere, anywhere, anywhere, inside, anywhere, anywhere, anywhere],
        out_specs=(anywhere, inside),
        scratch_shapes=[
            tokens, tokens, tokens,
            pltpu.VMEM((2, 128, 4096), BF16),
            pltpu.VMEM((2, 8, 128, 512), BF16),
            pltpu.VMEM((3, 512, 512), F32),
            pltpu.VMEM((3, 2, 16, 512), F32),
            pltpu.VMEM((3, 3, 512, 512), BF16),
            plain, wide, wide, plain, plain,
            pltpu.VMEM((3, 512, 512), F32),
            pltpu.VMEM((2, 3, 512, 512), BF16),
            pltpu.VMEM((2, 3, 2, 3, 64, 512), BF16),
            pltpu.VMEM((3, 2, 64, 512), F32),
            pltpu.VMEM((2, 3, 2, 64, 512), BF16),
            pltpu.VMEM((2, 3, 2, 3, 16, 512), BF16),
            pltpu.VMEM((3, 512, 512), BF16),
            tokens,
            dma((2, 3, 7)), dma((2, 3, 7)),
            dma((2, 7)), dma((2, 7)),
            dma((2, 3, 2, 3)), dma((2, 3, 2, 3)),
            dma((2, 3, 2, 3)), dma((2, 3, 2, 3)),
            dma((2, 3, 2, 3)), dma((2, 3, 2, 3)),
            dma((2, 3, 2, 3)), dma((2, 3, 2, 3)),
            dma((2,)), dma((2,)),
            dma((2, 3)), dma((2, 3)),
            dma((2, 3)), dma((2, 3)),
            dma((11,)),
        ],
        compiler_params=pltpu.CompilerParams(
            collective_id=0, has_side_effects=True, vmem_limit_bytes=60 << 20
        ),
    )(queries, memory_keys, memory_values, jnp.swapaxes(rates, 1, 2), fast_gate, fast_up, fast_down)
    return out, *[lax.index_in_dim(fin, n, 0, keepdims=False).astype(F32) for n in range(3)]


def solution(mesh):
    tokens = P(None, ("seq", "head"), None)
    heads = P("head", None, None)
    return jax.shard_map(
        on_device,
        mesh=mesh,
        in_specs=(tokens, tokens, tokens, tokens, heads, heads, heads),
        out_specs=(tokens, heads, heads, heads),
        check_vma=False,
    )
```

```python
import jax
import jax.numpy as jnp
from jax import lax
from jax.experimental import pallas as pl
from jax.experimental.pallas import tpu as pltpu
from jax.sharding import PartitionSpec as P

EPSILON = 1e-06
MESH = pl.DeviceIdType.MESH
F32 = jnp.float32
BF16 = jnp.bfloat16
GATE, UP, DOWN = 0, 1, 2
NEAR = (2, 1, 3)


def nt(a, b):
    return lax.dot_general(a, b, (((1,), (1,)), ((), ())), preferred_element_type=F32)


def nn(a, b):
    return lax.dot_general(a, b, (((1,), (0,)), ((), ())), preferred_element_type=F32)


def tn(a, b):
    return lax.dot_general(a, b, (((0,), (0,)), ((), ())), preferred_element_type=F32)


def device(x, y, z, core):
    return {"seq": x * 8 + (y // 2) * 4 + z, "head": (y % 2) * 2 + core}


def head_of(y, core):
    return 4 * (y % 2) + 2 * core + y // 2


def kernel(
    q, k, v, r, g, u, w, out, fin,
    kb, tb, qb, vb, tl, wf, st, wt, hid, ga, gb, da, db, gf, gs, r1, pf, s2, r2, wo, ob,
    tok_s, tok_r, out_s, out_r, rs1_s, rs1_r, rs2_s, rs2_r, ag1_s, ag1_r, ag2_s, ag2_r,
    fx_s, fx_r, fa1_s, fa1_r, fa2_s, fa2_r, loc,
):
    seq, hd = lax.axis_index("seq"), lax.axis_index("head")
    x, z = seq // 8, seq % 4
    y = ((seq // 4) % 2) * 2 + hd // 2
    core = hd % 2
    me = y * 2 + core
    head = head_of(y, core)
    sends = []

    def put(src, dst, ssem, rsem, where):
        copy = pltpu.make_async_remote_copy(
            src_ref=src, dst_ref=dst, send_sem=ssem, recv_sem=rsem, device_id=where, device_id_type=MESH
        )
        copy.start()
        sends.append(copy)
        return copy

    def local(src, dst, n):
        copy = pltpu.make_async_copy(src, dst, loc.at[n])
        copy.start()
        return copy

    def cols(h):
        return pl.ds(pl.multiple_of(h * 512, 512), 512)

    def rows(start, size):
        return pl.ds(pl.multiple_of(start, size), size)

    own_v = [local(v.at[c], vb.at[c], c) for c in range(2)]
    own_w = [local(m.at[y // 2], wf.at[n], 2 + n) for n, m in enumerate((g, u, w))]
    own_k = [local(k.at[c, :, cols(head)], kb.at[c, rows(me * 128, 128), :], 5 + c) for c in range(2)]
    own_q = [local(q.at[c, :, cols(head)], qb.at[c, rows(me * 128, 128), :], 7 + c) for c in range(2)]

    group = [(dy, dc) for dy in NEAR for dc in range(2)] + [(0, 1)]
    friends = [device(x, (y + dy) % 4, z, (core + dc) % 2) for dy, dc in group]
    friends += [device((x + d) % 4, y, z, core) for d in NEAR]
    friends += [device(x, y, (z + d) % 4, core) for d in NEAR]
    barrier = pltpu.get_barrier_semaphore()
    for where in friends:
        pl.semaphore_signal(barrier, inc=1, device_id=where, device_id_type=MESH)
    pl.semaphore_wait(barrier, len(friends))

    def send_tokens(c, kind, source, held):
        copies = []
        for dy, dc in group:
            y2, core2 = (y + dy) % 4, (core + dc) % 2
            n = dy * 2 + dc - 1
            copies.append(
                put(
                    source(head_of(y2, core2)),
                    held.at[c, rows(me * 128, 128), :],
                    tok_s.at[c, kind, n],
                    tok_r.at[c, kind, n],
                    device(x, y2, z, core2),
                )
            )
        return copies

    def targets(c):
        rate = r[c].T
        own_v[c].wait()
        for h in range(8):
            tl[c, h] = (-rate[:, h : h + 1] * vb[c, :, h * 512 : (h + 1) * 512].astype(F32)).astype(BF16)
        tb[c, rows(me * 128, 128), :] = tl[c, head]

    got_k, got_t, got_q = [None, None], [None, None], [None, None]
    for c in range(2):
        got_k[c] = send_tokens(c, 0, lambda h: k.at[c, :, cols(h)], kb)
        targets(c)
        got_t[c] = send_tokens(c, 1, lambda h: tl.at[c, h], tb)
    for c in range(2):
        got_q[c] = send_tokens(c, 2, lambda h: q.at[c, :, cols(h)], qb)

    first = (x, z)
    second = (z, x)
    share = [256 * p + 64 * first[p] + 16 * second[p] for p in range(2)]

    def along(p, phase, d):
        if (p + phase) % 2 == 0:
            return device((x + d) % 4, y, z, core)
        return device(x, y, (z + d) % 4, core)

    for n in range(3):
        own_w[n].wait()
        turned = wf[n].T
        gf[n] = turned
        wt[0, n] = turned.astype(BF16)
        for p in range(2):
            st[n, p] = gf[n, rows(share[p], 16), :]

    def reduce_out(c, m, p):
        copies = []
        for d in NEAR:
            src = gs.at[c, m, rows(256 * p + 64 * ((first[p] + d) % 4), 64), :]
            copies.append(
                put(src, r1.at[c, m, p, d - 1], rs1_s.at[c, m, p, d - 1], rs1_r.at[c, m, p, d - 1], along(p, 0, d))
            )
        return copies

    def reduce_mid(c, m, p, waits):
        for copy in waits:
            copy.wait_recv()
        total = gf[m, rows(256 * p + 64 * first[p], 64), :]
        for d in range(3):
            total = total + r1[c, m, p, d].astype(F32)
        pf[m, p] = total
        s2[c, m, p] = total.astype(BF16)
        copies = []
        for d in NEAR:
            src = s2.at[c, m, p, rows(16 * ((second[p] + d) % 4), 16), :]
            copies.append(
                put(src, r2.at[c, m, p, d - 1], rs2_s.at[c, m, p, d - 1], rs2_r.at[c, m, p, d - 1], along(p, 1, d))
            )
        return copies

    def update(c, m, p, waits):
        for copy in waits:
            copy.wait_recv()
        grad = pf[m, p, rows(16 * second[p], 16), :]
        for d in range(3):
            grad = grad + r2[c, m, p, d].astype(F32)
        old = st[m, p]
        new = old - grad
        old_norm = jnp.sqrt(jnp.sum(old * old, axis=1, keepdims=True) + EPSILON)
        new_norm = jnp.sqrt(jnp.sum(new * new, axis=1, keepdims=True) + EPSILON)
        new = new * (old_norm / new_norm)
        st[m, p] = new
        part = rows(share[p], 16)
        wt[c + 1, m, part, :] = new.astype(BF16)
        copies = []
        for d in NEAR:
            piece = wt.at[c + 1, m, part, :]
            copies.append(put(piece, piece, ag1_s.at[c, m, p, d - 1], ag1_r.at[c, m, p, d - 1], along(p, 1, d)))
        return copies

    def spread(c, m, p, waits):
        for copy in waits:
            copy.wait_recv()
        copies = []
        for d in NEAR:
            piece = wt.at[c + 1, m, rows(256 * p + 64 * first[p], 64), :]
            copies.append(put(piece, piece, ag2_s.at[c, m, p, d - 1], ag2_r.at[c, m, p, d - 1], along(p, 0, d)))
        return copies

    def both(step, c, m, waits=None):
        if waits is None:
            return [step(c, m, p) for p in range(2)]
        return [step(c, m, p, waits[p]) for p in range(2)]

    def arrived(copies):
        for part in copies:
            for copy in part:
                copy.wait_recv()

    def forward(c):
        own_k[c].wait()
        for copy in got_k[c]:
            copy.wait_recv()

        def block(i, _):
            part = rows(i * 256, 256)
            keys = kb[c, part, :]
            a = nt(keys, wt[c, GATE])
            b = nt(keys, wt[c, UP])
            s = jax.nn.sigmoid(a)
            act = a * s
            hid[part, :] = (act * b).astype(BF16)
            ga[part, :] = b * s * (1.0 + a * (1.0 - s))
            gb[part, :] = act
            return 0

        lax.fori_loop(0, 4, block, 0)

    def grad_half(c, m, p, left, right):
        res = tn(left[:, 256 * p : 256 * (p + 1)], right)
        gf[m, 256 * p : 256 * (p + 1), :] = res
        gs[c, m, 256 * p : 256 * (p + 1), :] = res.astype(BF16)
        return reduce_out(c, m, p)

    def deltas(c):
        def block(i, _):
            part = rows(i * 256, 256)
            dh = nn(tb[c, part, :], wt[c, DOWN])
            da[part, :] = (dh * ga[part, :]).astype(BF16)
            db[part, :] = (dh * gb[part, :]).astype(BF16)
            return 0

        lax.fori_loop(0, 4, block, 0)

    kept = []

    def apply_block(c, dy):
        y2 = (y + dy) % 4
        part = rows(256 * y2, 256)
        queries = qb[c, part, :]
        p = nt(queries, wt[c + 1, GATE])
        u2 = nt(queries, wt[c + 1, UP])
        hidden = (p * jax.nn.sigmoid(p) * u2).astype(BF16)
        ob[c, part, :] = nt(hidden, wt[c + 1, DOWN]).astype(BF16)
        copies = []
        for dc in range(2):
            core2 = (core + dc) % 2
            tile = ob.at[c, rows(256 * y2 + 128 * core2, 128), :]
            place = out.at[c, :, cols(head)]
            if dy == 0 and dc == 0:
                kept.append(local(tile, place, 9 + c))
            else:
                n = dy * 2 + dc - 1
                copies.append(put(tile, place, out_s.at[c, n], out_r.at[c, n], device(x, y2, z, core2)))
        return copies

    got_out = []

    def apply_all(c):
        own_q[c].wait()
        for copy in got_q[c]:
            copy.wait_recv()
        for dy in NEAR + (0,):
            got_out.extend(apply_block(c, dy))

    def other_exchange():
        copies = []
        for p in range(2):
            part = rows(share[p], 16)
            copies.append(
                put(wt.at[2, :, part, :], wo.at[:, part, :], fx_s.at[p], fx_r.at[p], device(x, (y + 2) % 4, z, core))
            )
        return copies

    def other_first(waits):
        copies = []
        for p in range(2):
            waits[p].wait_recv()
            piece = wo.at[:, rows(share[p], 16), :]
            copies.append(
                [put(piece, piece, fa1_s.at[p, d - 1], fa1_r.at[p, d - 1], along(p, 1, d)) for d in NEAR]
            )
        return copies

    def other_second(waits):
        copies = []
        for p in range(2):
            for copy in waits[p]:
                copy.wait_recv()
            piece = wo.at[:, rows(256 * p + 64 * first[p], 64), :]
            copies.append(
                [put(piece, piece, fa2_s.at[p, d - 1], fa2_r.at[p, d - 1], along(p, 0, d)) for d in NEAR]
            )
        return copies

    def ready(c):
        if c == 1:
            own_q[0].wait()
            for copy in got_q[0]:
                copy.wait_recv()

    def piece_of(c, dy):
        if c == 1:
            got_out.extend(apply_block(0, dy))

    for c in range(2):
        forward(c)
        for copy in got_t[c]:
            copy.wait_recv()
        w1 = [grad_half(c, DOWN, p, tb.at[c], hid[...]) for p in range(2)]
        deltas(c)
        g1 = [grad_half(c, GATE, p, da, kb[c]) for p in range(2)]
        w2 = both(reduce_mid, c, DOWN, w1)
        u1 = [grad_half(c, UP, p, db, kb[c]) for p in range(2)]
        ready(c)
        g2 = both(reduce_mid, c, GATE, g1)
        piece_of(c, 2)
        w3 = both(update, c, DOWN, w2)
        piece_of(c, 1)
        u2 = both(reduce_mid, c, UP, u1)
        piece_of(c, 3)
        g3 = both(update, c, GATE, g2)
        piece_of(c, 0)
        w4 = both(spread, c, DOWN, w3)
        u3 = both(update, c, UP, u2)
        if c == 1:
            fx = other_exchange()
        g4 = both(spread, c, GATE, g3)
        u4 = both(spread, c, UP, u3)
        if c == 1:
            f1 = other_first(fx)
        arrived(g4)
        arrived(u4)
        arrived(w4)
    apply_all(1)
    f2 = other_second(f1)
    for n in range(3):
        fin[n, y // 2] = wt[2, n].astype(F32).T.astype(BF16)
    arrived(f2)
    for n in range(3):
        fin[n, 1 - y // 2] = wo[n].astype(F32).T.astype(BF16)
    for copy in got_out:
        copy.wait_recv()
    for copy in kept:
        copy.wait()
    for copy in sends:
        copy.wait_send()


def on_device(queries, memory_keys, memory_values, rates, fast_gate, fast_up, fast_down):
    anywhere = pl.BlockSpec(memory_space=pl.ANY)
    inside = pl.BlockSpec(memory_space=pltpu.VMEM)
    dma = pltpu.SemaphoreType.DMA
    tokens = pltpu.VMEM((2, 1024, 512), BF16)
    plain = pltpu.VMEM((1024, 512), BF16)
    wide = pltpu.VMEM((1024, 512), F32)
    out, fin = pl.pallas_call(
        kernel,
        name="fast_weights",
        out_shape=(
            jax.ShapeDtypeStruct((2, 128, 4096), BF16),
            jax.ShapeDtypeStruct((3, 2, 512, 512), BF16),
        ),
        in_specs=[anywhere, anywhere, anywhere, inside, anywhere, anywhere, anywhere],
        out_specs=(anywhere, inside),
        scratch_shapes=[
            tokens, tokens, tokens,
            pltpu.VMEM((2, 128, 4096), BF16),
            pltpu.VMEM((2, 8, 128, 512), BF16),
            pltpu.VMEM((3, 512, 512), F32),
            pltpu.VMEM((3, 2, 16, 512), F32),
            pltpu.VMEM((3, 3, 512, 512), BF16),
            plain, wide, wide, plain, plain,
            pltpu.VMEM((3, 512, 512), F32),
            pltpu.VMEM((2, 3, 512, 512), BF16),
            pltpu.VMEM((2, 3, 2, 3, 64, 512), BF16),
            pltpu.VMEM((3, 2, 64, 512), F32),
            pltpu.VMEM((2, 3, 2, 64, 512), BF16),
            pltpu.VMEM((2, 3, 2, 3, 16, 512), BF16),
            pltpu.VMEM((3, 512, 512), BF16),
            tokens,
            dma((2, 3, 7)), dma((2, 3, 7)),
            dma((2, 7)), dma((2, 7)),
            dma((2, 3, 2, 3)), dma((2, 3, 2, 3)),
            dma((2, 3, 2, 3)), dma((2, 3, 2, 3)),
            dma((2, 3, 2, 3)), dma((2, 3, 2, 3)),
            dma((2, 3, 2, 3)), dma((2, 3, 2, 3)),
            dma((2,)), dma((2,)),
            dma((2, 3)), dma((2, 3)),
            dma((2, 3)), dma((2, 3)),
            dma((11,)),
        ],
        compiler_params=pltpu.CompilerParams(
            collective_id=0, has_side_effects=True, vmem_limit_bytes=60 << 20
        ),
    )(queries, memory_keys, memory_values, jnp.swapaxes(rates, 1, 2), fast_gate, fast_up, fast_down)
    return out, *[lax.index_in_dim(fin, n, 0, keepdims=False).astype(F32) for n in range(3)]


def solution(mesh):
    tokens = P(None, ("seq", "head"), None)
    heads = P("head", None, None)
    return jax.shard_map(
        on_device,
        mesh=mesh,
        in_specs=(tokens, tokens, tokens, tokens, heads, heads, heads),
        out_specs=(tokens, heads, heads, heads),
        check_vma=False,
    )
```
